256 devices in a mesh: region: 32 (over x, z), group: 8 (over y, core).
Axes of the slice: x: 4, y: 4, z: 8, core: 2. Of those that a mesh axis runs over, the one named last changes fastest.
Arguments:
- block_coords: int32 [8, 192, 3], P('group', 'region'), may hold values from -100 to 63, as said below
- features: bfloat16 [8, 192, 8, 8, 8, 128], P('group', 'region'), may hold values from -6 to 6
- cotangent: bfloat16 [8, 192, 4, 4, 4, 128], P('group', 'region'), may hold values from -6 to 6
- weights: bfloat16 [3, 3, 3, 128, 128], replicated, may hold values from -0.109375 to 0.109375
Outputs:
- coarse_features: bfloat16 [8, 192, 4, 4, 4, 128], P('group', 'region')
- grad_features: bfloat16 [8, 192, 8, 8, 8, 128], P('group', 'region')
- grad_weight: float32 [3, 3, 3, 128, 128], replicated
The draws below stay inside these ranges and needn't reach their ends.
Inputs may be any that keep to these rules, and one draw needn't show every extreme that they name: `block_coords`: slot s of device r along region holds a block with coordinates (x, y, z), x being 2r or 2r+1, 0 <= y < 1, 0 <= z < 4; a device's blocks are distinct; its occupied slots come first and the others hold -100 in all three coordinates; every device holds 3 to 6 blocks, and in each map one device holds 6 and another 6 // 2.
All inputs are finite; a program needn't handle non-finite values.
Results may differ from the reference program's by a relative error of at most 0.0023.
Values may be sent and summed in bfloat16 or wider, within the bound.
No kernel may reach another device: no remote copies, remote signals or barrier semaphores. Data moves between devices by JAX's collectives and lax.ppermute only.
A program may use at most 64 MiB of HBM per device.

```python
import math
import jax
import jax.numpy as jnp
from jax import lax

C = 128
BLOCK = 8
CROSS_Y = 1
CROSS_Z = 4
BLK_DEV = 6
SLOTS = 192
TILES = 8
N_REGION = 32


def slab_draw(slab_key, count, top_count, region_number):
    sub_keys = jax.random.split(slab_key, 3)
    cell_count = CROSS_Y * CROSS_Z
    top_cells = jax.random.permutation(sub_keys[0], cell_count).astype(jnp.int32)
    low_cells = jax.random.permutation(sub_keys[1], cell_count).astype(jnp.int32)
    shuffle = jax.random.permutation(sub_keys[2], BLK_DEV).astype(jnp.int32)
    item_ids = jnp.arange(BLK_DEV, dtype=jnp.int32)
    in_top = item_ids < top_count
    cell_index = jnp.where(in_top, top_cells[jnp.minimum(item_ids, cell_count - 1)], low_cells[jnp.clip(item_ids - top_count, 0, cell_count - 1)])
    layer_index = jnp.where(in_top, 1, 0)
    coords = jnp.stack([2 * region_number + layer_index, cell_index // CROSS_Z, cell_index % CROSS_Z], axis=1)
    coords = jnp.where((item_ids < count)[:, None], coords, -100)
    order_keys = jnp.where(shuffle < count, item_ids, BLK_DEV + item_ids)
    slot_order = jnp.argsort(order_keys)
    return coords[shuffle[slot_order]].astype(jnp.int32)


def draw_block_coords(key, part):
    regions = SLOTS // BLK_DEV
    key_count, key_full, key_sparse, key_top, key_slabs = jax.random.split(key, 5)
    counts = jax.random.randint(key_count, (TILES, regions), BLK_DEV // 2, BLK_DEV + 1)
    full_at = jax.random.randint(key_full, (TILES, 1), 0, regions)
    sparse_at = (full_at + 1 + jax.random.randint(key_sparse, (TILES, 1), 0, regions - 1)) % regions
    region_ranks = jnp.arange(regions)[None, :]
    counts = jnp.where(region_ranks == full_at, BLK_DEV, jnp.where(region_ranks == sparse_at, BLK_DEV // 2, counts))
    cell_count = CROSS_Y * CROSS_Z
    low_bound = jnp.maximum(counts - cell_count, counts // 3)
    high_bound = jnp.minimum(counts, cell_count)
    top_counts = jax.random.randint(key_top, (TILES, regions), low_bound, high_bound + 1)
    slab_keys = jax.random.split(key_slabs, TILES * regions)
    region_numbers = jnp.tile(jnp.arange(regions, dtype=jnp.int32), TILES)
    result = jax.vmap(slab_draw)(slab_keys, counts.reshape(-1).astype(jnp.int32), top_counts.reshape(-1).astype(jnp.int32), region_numbers)
    return result.reshape(TILES, SLOTS, 3).astype(jnp.int32)


def steps_of(key, dims, cuts, low, high):
    factor_of = 1.0
    for position, blocks in cuts:
        steps = jax.random.uniform(jax.random.fold_in(jax.random.fold_in(key, 6), position), (blocks,), jnp.float32, low / len(cuts), high / len(cuts))
        factor_of = factor_of * jnp.repeat(jnp.exp(steps), dims[position] // blocks).reshape((-1,) + (1,) * (len(dims) - 1 - position))
    return factor_of


def bell_draw(own_key, extent, spread, most, cuts=(), kind=jnp.bfloat16):
    gain = steps_of(own_key, extent, cuts, -0.22, 0.18) if cuts else 1.0
    entries = jax.random.normal(own_key, extent, jnp.float32) * spread * gain
    return jnp.minimum(jnp.maximum(entries, -most), most).astype(kind)


def setup_inputs(seed: int = 0) -> dict:
    key_list = jax.random.split(jax.random.key(seed), 5)
    return {
        "block_coords": draw_block_coords(jax.random.fold_in(key_list[4], 71), 0),
        "features": bell_draw(key_list[1], (TILES, SLOTS, BLOCK, BLOCK, BLOCK, C), 1.0, 6.0, ((0, 8), (1, 32))),
        "cotangent": bell_draw(key_list[2], (TILES, SLOTS, BLOCK // 2, BLOCK // 2, BLOCK // 2, C), 1.0, 6.0, ((0, 8), (1, 32))),
        "weights": bell_draw(key_list[3], (3, 3, 3, C, C), (27 * C) ** -0.5, 0.109375),
    }


LOWER_SIDES = ((-1, 0, 0), (-1, -1, 0), (-1, 0, -1), (-1, -1, -1), (0, -1, 0), (0, 0, -1), (0, -1, -1))

def unfold(volume, which_axis):
    pieces = [lax.slice_in_dim(volume, offset, offset + 7, 2, which_axis) for offset in range(3)]
    return jnp.stack(pieces, axis=which_axis + 1)

def fold_back(col_terms, which_axis):
    lower_part, middle_part, upper_part = [lax.index_in_dim(col_terms, offset, which_axis + 1, keepdims=False) for offset in range(3)]
    zero_row = jnp.zeros_like(lax.slice_in_dim(lower_part, 0, 1, 1, which_axis))
    even_rows = jnp.concatenate([lower_part, zero_row], which_axis) + jnp.concatenate([zero_row, upper_part], which_axis)
    paired = jnp.stack([lax.slice_in_dim(even_rows, 0, 4, 1, which_axis), middle_part], which_axis + 1)
    new_shape = list(lower_part.shape)
    new_shape[which_axis] = 8
    merged = paired.reshape(new_shape)
    return jnp.concatenate([merged, lax.slice_in_dim(even_rows, 4, 5, 1, which_axis)], which_axis)

def pick_rows(lookup_table, link):
    safe_rows = jnp.clip(link[0], 0, lookup_table.shape[0] - 1)
    gathered = jnp.take(lookup_table, safe_rows, axis=0)
    present_mask = link[1].reshape((-1,) + (1,) * (gathered.ndim - 1))
    return jnp.where(present_mask, gathered, jnp.zeros_like(gathered))

def assemble(blocks, planes, source_links):
    face_x = pick_rows(planes, source_links[0])
    edge_xy = pick_rows(planes[:, 7], source_links[1])
    edge_xz = pick_rows(planes[:, :, 7], source_links[2])
    corner = pick_rows(planes[:, 7, 7], source_links[3])
    face_y = pick_rows(blocks[:, :, 7], source_links[4])
    face_z = pick_rows(blocks[:, :, :, 7], source_links[5])
    edge_yz = pick_rows(blocks[:, :, 7, 7], source_links[6])
    first_plane = jnp.concatenate([jnp.concatenate([corner[:, None, None], edge_xy[:, None]], axis=2), jnp.concatenate([edge_xz[:, :, None], face_x], axis=2)], axis=1)
    low_row = jnp.concatenate([edge_yz[:, :, None], face_y], axis=2)[:, :, None]
    interior = jnp.concatenate([face_z[:, :, :, None], blocks], axis=3)
    upper_part = jnp.concatenate([low_row, interior], axis=2)
    return jnp.concatenate([first_plane[:, None], upper_part], axis=1)

def aim_rows(link, limit):
    return jnp.where(link[1], link[0], limit).astype(jnp.int32)

def spread_rims(ext_grads, source_links, block_count, table_rows):
    own_grad = ext_grads[:, 1:, 1:, 1:]
    planes = jnp.zeros((table_rows,) + own_grad.shape[2:], ext_grads.dtype)
    planes = planes.at[aim_rows(source_links[0], table_rows)].add(ext_grads[:, 0, 1:, 1:], mode='drop')
    planes = planes.at[aim_rows(source_links[1], table_rows), 7].add(ext_grads[:, 0, 0, 1:], mode='drop')
    planes = planes.at[aim_rows(source_links[2], table_rows), :, 7].add(ext_grads[:, 0, 1:, 0], mode='drop')
    planes = planes.at[aim_rows(source_links[3], table_rows), 7, 7].add(ext_grads[:, 0, 0, 0], mode='drop')
    own_grad = own_grad.at[aim_rows(source_links[4], block_count), :, 7].add(ext_grads[:, 1:, 0, 1:], mode='drop')
    own_grad = own_grad.at[aim_rows(source_links[5], block_count), :, :, 7].add(ext_grads[:, 1:, 1:, 0], mode='drop')
    own_grad = own_grad.at[aim_rows(source_links[6], block_count), :, 7, 7].add(ext_grads[:, 1:, 0, 0], mode='drop')
    return (own_grad, planes)

def find_links(coords):
    block_count = coords.shape[0]
    slot_ids = jnp.arange(block_count, dtype=jnp.int32)
    collected = []
    for side in LOWER_SIDES:
        wanted = coords + jnp.array(side, jnp.int32)
        matches = jnp.all(wanted[:, None, :] == coords[None, :, :], axis=2)
        present = jnp.any(matches, axis=1)
        source = lax.optimization_barrier(jnp.sum(jnp.where(matches, slot_ids[None, :], 0), axis=1)).astype(jnp.int32)
        collected.append((source, present))
    return collected

def by_batches(volume):
    return volume.reshape((N_REGION, BLK_DEV) + volume.shape[1:])

def tile_result(coords, feats, upstream, weights):
    block_count = coords.shape[0]
    source_links = find_links(coords)
    extended = assemble(feats, feats[:, 7], source_links)
    occupied = coords[:, 0] >= 0
    block_mask = occupied[:, None, None, None, None]
    masked = jnp.where(block_mask, upstream, jnp.zeros_like(upstream))
    wide_weights = weights.astype(jnp.float32)

    def batch_work(batch_data):
        ext_part, cot_part, mask_part = batch_data
        columns = unfold(unfold(unfold(ext_part, 1), 3), 5).astype(jnp.float32)
        cot_wide = cot_part.astype(jnp.float32)
        result = jnp.einsum('nxaybzcf,abcfo->nxyzo', columns, wide_weights)
        result = jnp.where(mask_part, result, 0.0)
        weight_part = jnp.einsum('nxaybzcf,nxyzo->abcfo', columns, cot_wide)
        col_terms = jnp.einsum('nxyzo,abcfo->nxaybzcf', cot_wide, wide_weights)
        ext_grads = fold_back(fold_back(fold_back(col_terms, 5), 3), 1)
        return (result, ext_grads, weight_part)
    results, ext_grads, weight_parts = lax.map(batch_work, (by_batches(extended), by_batches(masked), by_batches(block_mask)))
    results = results.reshape((block_count,) + results.shape[2:])
    ext_grads = ext_grads.reshape((block_count,) + ext_grads.shape[2:])
    own_grad, plane_grads = spread_rims(ext_grads, source_links, block_count, block_count)
    own_grad = own_grad.at[:, 7].add(plane_grads)
    return (results.astype(jnp.bfloat16), own_grad.astype(jnp.bfloat16), lax.optimization_barrier(jnp.sum(weight_parts, axis=0)))

def reference(block_coords, features, cotangent, weights):

    def per_tile(tile_data):
        return tile_result(tile_data[0], tile_data[1], tile_data[2], weights)
    coarse, grad_in, weight_parts = lax.map(per_tile, (block_coords, features, cotangent))
    grad_weight = lax.optimization_barrier(jnp.sum(weight_parts, axis=0)) * (1.0 / math.sqrt(TILES * SLOTS * 64))
    return (coarse, grad_in, grad_weight)
```

```python
import math

import jax
import jax.numpy as jnp
from jax import lax
from jax.sharding import Mesh
from jax.sharding import PartitionSpec as P

CROSS_Y = 1
CROSS_Z = 4
REGION = ("x", "z")
GROUP = ("y", "core")


LOWER_SIDES = (
    (-1, 0, 0),
    (-1, -1, 0),
    (-1, 0, -1),
    (-1, -1, -1),
    (0, -1, 0),
    (0, 0, -1),
    (0, -1, -1),
)


def shifted(block, axis, distance):
    devices = range(lax.axis_size(axis))
    route = [(i - distance, i) for i in devices if i - distance in devices]
    return lax.ppermute(block, axis, route)


def ring(x, axis, distance):
    n = lax.axis_size(axis)
    return lax.ppermute(x, axis, [(i, (i + distance) % n) for i in range(n)])


def scatter_sum(parts, axis):
    n = lax.axis_size(axis)
    me = lax.axis_index(axis)
    arrived = [
        ring(lax.dynamic_index_in_dim(parts, (me + d) % n, 0, False), axis, d)
        for d in range(1, n)
    ]
    total = lax.dynamic_index_in_dim(parts, me, 0, False)
    for piece in arrived:
        total = total + piece
    return total


def gather(piece, axis):
    n = lax.axis_size(axis)
    me = lax.axis_index(axis)
    whole = jnp.zeros((n,) + piece.shape, piece.dtype)
    whole = lax.dynamic_update_index_in_dim(whole, piece, me, 0)
    for d in range(1, n):
        whole = lax.dynamic_update_index_in_dim(whole, ring(piece, axis, d), (me - d) % n, 0)
    return whole


def reduce_everywhere(partial, scale):
    rows = partial.shape[0]
    cores, ys, xs, zs = (lax.axis_size(a) for a in ("core", "y", "x", "z"))
    per_y = rows // (cores * ys)
    padded = -(-per_y // (8 * xs)) * 8 * xs
    half = scatter_sum(partial.reshape(cores, ys * per_y, 128), "core")
    mine = scatter_sum(half.reshape(ys, per_y, 128), "y")
    mine = jnp.pad(mine, ((0, padded - per_y), (0, 0)))
    mine = scatter_sum(mine.reshape(xs, padded // xs, 128), "x")
    along_z = lax.all_to_all(jnp.broadcast_to(mine[None], (zs,) + mine.shape), "z", 0, 0)
    total = (jnp.sum(along_z, axis=0) * scale).astype(jnp.bfloat16)
    whole = gather(total, "x").reshape(padded, 128)[:per_y]
    whole = gather(whole, "y").reshape(ys * per_y, 128)
    whole = gather(whole, "core").reshape(rows, 128)
    return whole.astype(jnp.float32)


def unfold(volume, which_axis):
    pieces = [lax.slice_in_dim(volume, offset, offset + 7, 2, which_axis) for offset in range(3)]
    return jnp.stack(pieces, axis=which_axis + 1)


def fold_back(col_terms, which_axis):
    lower_part, middle_part, upper_part = [
        lax.index_in_dim(col_terms, offset, which_axis + 1, keepdims=False) for offset in range(3)
    ]
    zero_row = jnp.zeros_like(lax.slice_in_dim(lower_part, 0, 1, 1, which_axis))
    even_rows = jnp.concatenate([lower_part, zero_row], which_axis) + jnp.concatenate(
        [zero_row, upper_part], which_axis
    )
    paired = jnp.stack(
        [lax.slice_in_dim(even_rows, 0, 4, 1, which_axis), middle_part], which_axis + 1
    )
    new_shape = list(lower_part.shape)
    new_shape[which_axis] = 8
    merged = paired.reshape(new_shape)
    return jnp.concatenate([merged, lax.slice_in_dim(even_rows, 4, 5, 1, which_axis)], which_axis)


def pick_rows(lookup_table, link):
    safe_rows = jnp.clip(link[0], 0, lookup_table.shape[0] - 1)
    gathered = jnp.take(lookup_table, safe_rows, axis=0)
    present_mask = link[1].reshape((-1,) + (1,) * (gathered.ndim - 1))
    return jnp.where(present_mask, gathered, jnp.zeros_like(gathered))


def assemble(blocks, planes, source_links):
    face_x = pick_rows(planes, source_links[0])
    edge_xy = pick_rows(planes[:, 7], source_links[1])
    edge_xz = pick_rows(planes[:, :, 7], source_links[2])
    corner = pick_rows(planes[:, 7, 7], source_links[3])
    face_y = pick_rows(blocks[:, :, 7], source_links[4])
    face_z = pick_rows(blocks[:, :, :, 7], source_links[5])
    edge_yz = pick_rows(blocks[:, :, 7, 7], source_links[6])
    first_plane = jnp.concatenate(
        [
            jnp.concatenate([corner[:, None, None], edge_xy[:, None]], axis=2),
            jnp.concatenate([edge_xz[:, :, None], face_x], axis=2),
        ],
        axis=1,
    )
    low_row = jnp.concatenate([edge_yz[:, :, None], face_y], axis=2)[:, :, None]
    interior = jnp.concatenate([face_z[:, :, :, None], blocks], axis=3)
    upper_part = jnp.concatenate([low_row, interior], axis=2)
    return jnp.concatenate([first_plane[:, None], upper_part], axis=1)


def aim_rows(link, limit):
    return jnp.where(link[1], link[0], limit)


def spread_rims(ext_grads, source_links, block_count, table_rows):
    own_grad = ext_grads[:, 1:, 1:, 1:]
    planes = jnp.zeros((table_rows,) + own_grad.shape[2:], ext_grads.dtype)
    planes = planes.at[aim_rows(source_links[0], table_rows)].add(
        ext_grads[:, 0, 1:, 1:], mode="drop"
    )
    planes = planes.at[aim_rows(source_links[1], table_rows), 7].add(
        ext_grads[:, 0, 0, 1:], mode="drop"
    )
    planes = planes.at[aim_rows(source_links[2], table_rows), :, 7].add(
        ext_grads[:, 0, 1:, 0], mode="drop"
    )
    planes = planes.at[aim_rows(source_links[3], table_rows), 7, 7].add(
        ext_grads[:, 0, 0, 0], mode="drop"
    )
    own_grad = own_grad.at[aim_rows(source_links[4], block_count), :, 7].add(
        ext_grads[:, 1:, 0, 1:], mode="drop"
    )
    own_grad = own_grad.at[aim_rows(source_links[5], block_count), :, :, 7].add(
        ext_grads[:, 1:, 1:, 0], mode="drop"
    )
    own_grad = own_grad.at[aim_rows(source_links[6], block_count), :, 7, 7].add(
        ext_grads[:, 1:, 0, 0], mode="drop"
    )
    return (own_grad, planes)


def find_links(coords, region_rank, block_count):
    slot_ids = jnp.arange(block_count, dtype=jnp.int32)
    collected = []
    for side in LOWER_SIDES:
        wanted = coords + jnp.array(side, jnp.int32)
        matches = jnp.all(wanted[:, None, :] == coords[None, :, :], axis=2)
        present = jnp.any(matches, axis=1)
        source = jnp.sum(jnp.where(matches, slot_ids[None, :], 0), axis=1)
        if side[0] == -1:
            remote = (
                (wanted[:, 0] == 2 * region_rank - 1)
                & (wanted[:, 1] >= 0)
                & (wanted[:, 1] < CROSS_Y)
                & (wanted[:, 2] >= 0)
                & (wanted[:, 2] < CROSS_Z)
            )
            source = jnp.where(present, source, block_count + wanted[:, 1] * CROSS_Z + wanted[:, 2])
            present = present | remote
        collected.append((source, present))
    return collected


def per_device(block_coords, features, cotangent, weights):
    coords = block_coords[0]
    blocks = features[0]
    upstream = cotangent[0]
    block_count = blocks.shape[0]
    cell_count = CROSS_Y * CROSS_Z
    region_rank = lax.axis_index(REGION)
    occupied = coords[:, 0] >= 0
    cell_index = coords[:, 1] * CROSS_Z + coords[:, 2]
    in_top = coords[:, 0] == 2 * region_rank + 1
    top_planes = blocks[:, 7]
    outgoing = (
        jnp.zeros((cell_count,) + top_planes.shape[1:], blocks.dtype)
        .at[jnp.where(in_top, cell_index, cell_count)]
        .set(top_planes, mode="drop")
    )
    incoming = shifted(outgoing, REGION, 1)
    source_links = find_links(coords, region_rank, block_count)
    plane_table = jnp.concatenate([top_planes, incoming], axis=0)
    extended = assemble(blocks, plane_table, source_links)
    columns = unfold(unfold(unfold(extended, 1), 3), 5)
    block_mask = occupied[:, None, None, None, None]
    result = jnp.einsum(
        "nxaybzcf,abcfo->nxyzo", columns, weights, preferred_element_type=jnp.float32
    )
    coarse = jnp.where(block_mask, result, 0.0).astype(jnp.bfloat16)
    masked = jnp.where(block_mask, upstream, jnp.zeros_like(upstream))
    local_grad = jnp.einsum(
        "nxaybzcf,nxyzo->abcfo", columns, masked, preferred_element_type=jnp.float32
    )
    col_terms = jnp.einsum(
        "nxyzo,abcfo->nxaybzcf", masked, weights, preferred_element_type=jnp.float32
    )
    ext_grads = fold_back(fold_back(fold_back(col_terms, 5), 3), 1)
    own_grad, plane_grads = spread_rims(
        ext_grads, source_links, block_count, block_count + cell_count
    )
    own_grad = own_grad.at[:, 7].add(plane_grads[:block_count])
    returned = shifted(plane_grads[block_count:].astype(jnp.bfloat16), REGION, -1).astype(
        jnp.float32
    )
    own_grad = own_grad.at[:, 7].add(pick_rows(returned, (cell_index, in_top)))
    grad_scale = 1.0 / math.sqrt(
        lax.axis_size(GROUP) * lax.axis_size(REGION) * block_count * upstream.shape[1] ** 3
    )
    summed = reduce_everywhere(local_grad.reshape(-1, 128), grad_scale).reshape(local_grad.shape)
    return (coarse[None], own_grad.astype(jnp.bfloat16)[None], summed)


def solution(mesh):
    mesh = Mesh(mesh.devices.reshape(4, 8, 4, 2), REGION + GROUP)
    return jax.shard_map(
        per_device,
        mesh=mesh,
        in_specs=(
            P(GROUP, REGION, None),
            P(GROUP, REGION, None, None, None, None),
            P(GROUP, REGION, None, None, None, None),
            P(),
        ),
        out_specs=(
            P(GROUP, REGION, None, None, None, None),
            P(GROUP, REGION, None, None, None, None),
            P(),
        ),
        check_vma=False,
    )
```

```python
import math

import jax
import jax.numpy as jnp
from jax import lax
from jax.sharding import Mesh
from jax.sharding import PartitionSpec as P

CROSS_Y = 1
CROSS_Z = 4
REGION = ("x", "z")
GROUP = ("y", "core")


def shifted(block, axis, distance):
    devices = range(lax.axis_size(axis))
    route = [(i - distance, i) for i in devices if i - distance in devices]
    return lax.ppermute(block, axis, route)


def ring(x, axis, distance):
    n = lax.axis_size(axis)
    return lax.ppermute(x, axis, [(i, (i + distance) % n) for i in range(n)])


def scatter_sum(parts, axis):
    n = lax.axis_size(axis)
    me = lax.axis_index(axis)
    arrived = [
        ring(lax.dynamic_index_in_dim(parts, (me + d) % n, 0, False), axis, d)
        for d in range(1, n)
    ]
    total = lax.dynamic_index_in_dim(parts, me, 0, False)
    for piece in arrived:
        total = total + piece
    return total


def gather(piece, axis):
    n = lax.axis_size(axis)
    me = lax.axis_index(axis)
    whole = jnp.zeros((n,) + piece.shape, piece.dtype)
    whole = lax.dynamic_update_index_in_dim(whole, piece, me, 0)
    for d in range(1, n):
        whole = lax.dynamic_update_index_in_dim(whole, ring(piece, axis, d), (me - d) % n, 0)
    return whole


def reduce_everywhere(partial, scale):
    rows = partial.shape[0]
    cores, ys, xs, zs = (lax.axis_size(a) for a in ("core", "y", "x", "z"))
    per_y = rows // (cores * ys)
    padded = -(-per_y // (8 * xs)) * 8 * xs
    half = scatter_sum(partial.reshape(cores, ys * per_y, 128), "core")
    mine = scatter_sum(half.reshape(ys, per_y, 128), "y")
    mine = jnp.pad(mine, ((0, padded - per_y), (0, 0)))
    mine = scatter_sum(mine.reshape(xs, padded // xs, 128), "x")
    along_z = lax.all_to_all(jnp.broadcast_to(mine[None], (zs,) + mine.shape), "z", 0, 0)
    total = (jnp.sum(along_z, axis=0) * scale).astype(jnp.bfloat16)
    whole = gather(total, "x").reshape(padded, 128)[:per_y]
    whole = gather(whole, "y").reshape(ys * per_y, 128)
    whole = gather(whole, "core").reshape(rows, 128)
    return whole.astype(jnp.float32)


def voxel_grid(cells):
    x, y, z, bx, by, bz, c = cells.shape
    return cells.transpose(0, 3, 1, 4, 2, 5, 6).reshape(x * bx, y * by, z * bz, c)


def pad_low(volume, axis):
    zero = jnp.zeros_like(lax.slice_in_dim(volume, 0, 1, 1, axis))
    return jnp.concatenate([zero, volume], axis)


def advance(volume, axis):
    rest = lax.slice_in_dim(volume, 1, volume.shape[axis], 1, axis)
    return jnp.concatenate([rest, jnp.zeros_like(lax.slice_in_dim(volume, 0, 1, 1, axis))], axis)


def taps(dense, incoming):
    extended = pad_low(jnp.concatenate([incoming[None], dense], 0), 1)
    nx, ny, nz, c = extended.shape
    pairs = extended.reshape(nx, ny, nz // 2, 2, c)
    even, odd = pairs[:, :, :, 0], pairs[:, :, :, 1]
    before = lax.slice_in_dim(pad_low(odd, 2), 0, nz // 2, 1, 2)
    return [
        along_z[kx : kx + nx - 2 : 2, ky : ky + ny - 2 : 2].reshape(-1, c)
        for kx in range(3)
        for ky in range(3)
        for along_z in (before, even, odd)
    ]


def input_grads(upstream, following, weights):
    sx, sy, sz, c = upstream.shape
    x_next = jnp.concatenate([upstream[1:], following[None]], 0)
    shifts = {}
    for ax, vx in enumerate((upstream, x_next)):
        for ay, vy in enumerate((vx, advance(vx, 1))):
            for az, vz in enumerate((vy, advance(vy, 2))):
                shifts[ax, ay, az] = vz.reshape(-1, c)
    choices = (((0, 1),), ((0, 2), (1, 0)))
    results = []
    for px in choices:
        for py in choices:
            for pz in choices:
                picked = [(x, y, z) for x in px for y in py for z in pz]
                left = jnp.concatenate([shifts[x[0], y[0], z[0]] for x, y, z in picked], 1)
                right = jnp.concatenate([weights[x[1], y[1], z[1]] for x, y, z in picked], 1)
                out = lax.dot_general(
                    left, right, (((1,), (1,)), ((), ())), preferred_element_type=jnp.float32
                )
                results.append(out.astype(jnp.bfloat16))
    return jnp.stack(results).reshape(2, 2, 2, sx, sy, sz, c)


def per_device(block_coords, features, cotangent, weights):
    coords = block_coords[0]
    blocks = features[0]
    upstream = cotangent[0]
    block_count, edge = blocks.shape[:2]
    half, c = edge // 2, blocks.shape[-1]
    grid = (2, CROSS_Y, CROSS_Z)
    cell_count = 2 * CROSS_Y * CROSS_Z
    region_rank = lax.axis_index(REGION)
    occupied = coords[:, 0] >= 0
    cell = ((coords[:, 0] - 2 * region_rank) * CROSS_Y + coords[:, 1]) * CROSS_Z + coords[:, 2]
    cell = jnp.where(occupied, cell, cell_count)
    holds = cell[None, :] == jnp.arange(cell_count, dtype=jnp.int32)[:, None]
    filled = jnp.any(holds, axis=1)[:, None, None, None, None]
    slot = jnp.sum(jnp.where(holds, jnp.arange(block_count, dtype=jnp.int32)[None, :], 0), axis=1)

    def to_cells(values):
        picked = jnp.take(values, slot, axis=0, mode="clip")
        picked = jnp.where(filled, picked, jnp.zeros_like(picked))
        return voxel_grid(picked.reshape(grid + values.shape[1:]))

    def to_slots(cells):
        picked = jnp.take(cells, cell, axis=0, mode="clip")
        return jnp.where(occupied[:, None, None, None, None], picked, jnp.zeros_like(picked))

    dense = to_cells(blocks)
    masked = to_cells(upstream)
    incoming = shifted(dense[-1], REGION, 1)
    following = shifted(masked[0], REGION, -1)
    columns = jnp.concatenate(taps(dense, incoming), 1)
    flat_masked = masked.reshape(-1, c)
    local_grad = lax.dot_general(
        columns, flat_masked, (((0,), (0,)), ((), ())), preferred_element_type=jnp.float32
    )
    grad_scale = 1.0 / math.sqrt(
        lax.axis_size(GROUP) * lax.axis_size(REGION) * block_count * upstream.shape[1] ** 3
    )
    summed = reduce_everywhere(local_grad, grad_scale).reshape(weights.shape)
    result = jnp.dot(columns, weights.reshape(-1, c), preferred_element_type=jnp.float32)
    coarse = result.astype(jnp.bfloat16).reshape(2, half, CROSS_Y, half, CROSS_Z, half, c)
    coarse = coarse.transpose(0, 2, 4, 1, 3, 5, 6).reshape((cell_count,) + upstream.shape[1:])
    grads = input_grads(masked, following, weights)
    grads = grads.reshape(2, 2, 2, 2, half, CROSS_Y, half, CROSS_Z, half, c)
    grads = grads.transpose(3, 5, 7, 4, 0, 6, 1, 8, 2, 9).reshape((cell_count,) + blocks.shape[1:])
    return (to_slots(coarse)[None], to_slots(grads)[None], summed)


def solution(mesh):
    mesh = Mesh(mesh.devices.reshape(4, 8, 4, 2), REGION + GROUP)
    return jax.shard_map(
        per_device,
        mesh=mesh,
        in_specs=(
            P(GROUP, REGION, None),
            P(GROUP, REGION, None, None, None, None),
            P(GROUP, REGION, None, None, None, None),
            P(),
        ),
        out_specs=(
            P(GROUP, REGION, None, None, None, None),
            P(GROUP, REGION, None, None, None, None),
            P(),
        ),
        check_vma=False,
    )
```
